512 devices in a mesh: grp: 16 (over z, y_lo), col: 32 (over x, y_hi, core).
Axes of the slice: x: 4, y: 8 (y_hi: 4, y_lo: 2; y = y_hi * 2 + y_lo), z: 8, core: 2. Of those that a mesh axis runs over, the one named last changes fastest.
Arguments:
- descriptors: bfloat16 [10, 32, 128, 4096], P(None, None, 'grp', 'col'), may hold values from -6 to 6
- solid_temp: float32 [32, 128, 4096], P(None, 'grp', 'col'), may hold values from -6 to 6
- fluid_temp: float32 [32, 128, 4096], P(None, 'grp', 'col'), may hold values from -6 to 6
- material: int32 [32, 128, 4096], P(None, 'grp', 'col'), may hold values from 0 to 3
- fixed_mask: int32 [32, 128, 4096], P(None, 'grp', 'col'), may hold values 0 or 1
- solid_cond: float32 [4], replicated, may hold values from 0.3 to 1.5
- fluid_cond: float32 [4], replicated, may hold values from 0.3 to 1.5
- w_in: bfloat16 [12, 64], replicated, may hold values from -1.75 to 1.75
- b_in: float32 [64], replicated, may hold values from -3 to 3
- w_mid: bfloat16 [64, 64], replicated, may hold values from -0.75 to 0.75
- b_mid: float32 [64], replicated, may hold values from -3 to 3
- w_out: bfloat16 [64, 2], replicated, may hold values from -0.75 to 0.75
- b_out: float32 [2], replicated, may hold values from -3 to 3
- solid_cot: float32 [32, 128, 4096], P(None, 'grp', 'col'), may hold values from -18 to 18
- fluid_cot: float32 [32, 128, 4096], P(None, 'grp', 'col'), may hold values from -18 to 18
Outputs:
- adj_solid: float32 [32, 128, 4096], P(None, 'grp', 'col')
- adj_fluid: float32 [32, 128, 4096], P(None, 'grp', 'col')
- grad_w_in: float32 [12, 64], replicated
- grad_b_in: float32 [64], replicated
- grad_w_mid: float32 [64, 64], replicated
- grad_b_mid: float32 [64], replicated
- grad_w_out: float32 [64, 2], replicated
- grad_b_out: float32 [2], replicated
The draws below stay inside these ranges and needn't reach their ends.
All inputs are finite; a program needn't handle non-finite values. No bound on the sum of `fixed_mask` on one device may be relied on, other than what follows from the above.
Results may differ from the reference program's by a relative error of at most 0.01.
The reference program's roundings to bfloat16 on the way (of `features`, `hidden_one`, `hidden_two` and `d_logits`) count: a program that leaves them out, or rounds other values in their place, can miss the bound.
Values sent between devices are 32-bit elements; how exact they have to be, the bound alone decides.
No kernel may reach another device: no remote copies, remote signals or barrier semaphores. Data moves between devices by JAX's collectives and lax.ppermute only.
A program may use at most 64 MiB of HBM per device.

```python
import math
import jax
import jax.numpy as jnp
from jax import lax

FEAT = 12
DESC = 10
HID = 64
NMAT = 4
NX = 128
NY = 4096
NZ = 32


def plant(result, own_key, least, largest):
    longest = result.shape.index(max(result.shape))
    spots = []
    for shift in (0, 1):
        where = [jax.random.randint(jax.random.fold_in(own_key, axis), (), 0, length) for axis, length in enumerate(result.shape)]
        where[longest] = (where[longest] + shift) % result.shape[longest]
        spots.append(tuple(where))
    return result.at[spots[0]].set(least).at[spots[1]].set(largest)


def steps_of(key, extent, pieces, least, top_value):
    def one(position, parts):
        draws = jax.random.uniform(jax.random.fold_in(jax.random.fold_in(key, 6), position), (parts,), jnp.float32, least / len(pieces), top_value / len(pieces))
        return jnp.repeat(jnp.exp(draws), extent[position] // parts).reshape((-1,) + (1,) * (len(extent) - position - 1))

    gain = one(*pieces[0])
    for cut in pieces[1:]:
        gain = gain * one(*cut)
    return gain


def scatter_about(key, dims, scale, reach, shards=(), kind=jnp.bfloat16):
    entries = scale * jax.random.normal(key, dims, jnp.float32)
    if shards:
        entries = entries * steps_of(key, dims, shards, -0.22, 0.18)
    return jnp.clip(entries, -reach, reach).astype(kind)


def setup_inputs(seed: int = 0) -> dict:
    splits = jax.random.split(jax.random.key(seed), 16)
    return {
        "descriptors": scatter_about(splits[0], (DESC, NZ, NX, NY), 1.0, 6.0, ((2, 16), (3, 32))),
        "solid_temp": scatter_about(splits[1], (NZ, NX, NY), 1.0, 6.0, ((1, 16), (2, 32)), jnp.float32),
        "fluid_temp": scatter_about(splits[2], (NZ, NX, NY), 1.0, 6.0, ((1, 16), (2, 32)), jnp.float32),
        "material": plant(jax.random.randint(splits[3], (NZ, NX, NY), 0, NMAT), jax.random.fold_in(splits[3], 1), 0, NMAT - 1).astype(jnp.int32),
        "fixed_mask": plant((jax.random.randint(splits[4], (NZ, NX, NY), 0, 8) < 1).astype(jnp.int32), jax.random.fold_in(splits[4], 1), 0, 1),
        "solid_cond": jnp.clip(jnp.exp(jax.random.uniform(splits[5], (NMAT,), jnp.float32, math.log(0.3), math.log(1.5))), 0.3, 1.5),
        "fluid_cond": jnp.clip(jnp.exp(jax.random.uniform(splits[6], (NMAT,), jnp.float32, math.log(0.3), math.log(1.5))), 0.3, 1.5),
        "w_in": scatter_about(splits[7], (FEAT, HID), FEAT ** -0.5, 1.75),
        "b_in": scatter_about(splits[8], (HID,), 0.5, 3.0, (), jnp.float32),
        "w_mid": scatter_about(splits[9], (HID, HID), HID ** -0.5, 0.75),
        "b_mid": scatter_about(splits[10], (HID,), 0.5, 3.0, (), jnp.float32),
        "w_out": scatter_about(splits[11], (HID, 2), HID ** -0.5, 0.75),
        "b_out": scatter_about(splits[12], (2,), 0.5, 3.0, (), jnp.float32),
        "solid_cot": scatter_about(splits[13], (NZ, NX, NY), 3.0, 18.0, ((1, 16), (2, 32)), jnp.float32),
        "fluid_cot": scatter_about(splits[14], (NZ, NX, NY), 3.0, 18.0, ((1, 16), (2, 32)), jnp.float32),
    }


time_step = 0.15
loss_gain = 16.0

def material_lookup(material, lookup_table):
    summed = jnp.zeros(material.shape, jnp.float32)
    for material_kind in range(lookup_table.shape[0]):
        summed = summed + jnp.where(material == material_kind, lookup_table[material_kind], 0.0)
    return summed

def neighbour_sum(padded, values_field):
    return padded[:, :, 2:, 1:-1] + padded[:, :, :-2, 1:-1] + padded[:, :, 1:-1, 2:] + padded[:, :, 1:-1, :-2] - 4.0 * values_field

def laplace(values_field):
    padded = jnp.pad(values_field, ((0, 0), (0, 0), (1, 1), (1, 1)))
    return neighbour_sum(padded, values_field)

def network(features, w_in, b_in, w_mid, b_mid, w_out, b_out):
    hidden_one = jnp.tanh(jnp.dot(w_in.T, features, preferred_element_type=jnp.float32) + b_in[:, None]).astype(jnp.bfloat16)
    hidden_two = jnp.tanh(jnp.dot(w_mid.T, hidden_one, preferred_element_type=jnp.float32) + b_mid[:, None]).astype(jnp.bfloat16)
    logits = jnp.dot(w_out.T, hidden_two, preferred_element_type=jnp.float32) + b_out[:, None]
    return (hidden_one, hidden_two, logits)

def coupling_terms(logits):
    transfer_coef = jax.nn.softplus(logits[0])
    area_coef = jax.nn.softplus(logits[1])
    return (transfer_coef * area_coef, transfer_coef, area_coef)

def backprop(features, hidden_one, hidden_two, logits, d_coupling, w_in, w_mid, w_out):
    coupling, transfer_coef, area_coef = coupling_terms(logits)
    d_logits = jnp.stack([d_coupling * area_coef * jax.nn.sigmoid(logits[0]), d_coupling * transfer_coef * jax.nn.sigmoid(logits[1])]).astype(jnp.bfloat16)
    d_hidden_two = (jnp.dot(w_out, d_logits, preferred_element_type=jnp.float32) * (1.0 - jnp.square(hidden_two.astype(jnp.float32)))).astype(jnp.bfloat16)
    d_hidden_one = (jnp.dot(w_mid, d_hidden_two, preferred_element_type=jnp.float32) * (1.0 - jnp.square(hidden_one.astype(jnp.float32)))).astype(jnp.bfloat16)
    d_features = jnp.dot(w_in[w_in.shape[0] - 2:], d_hidden_one, preferred_element_type=jnp.float32)
    gradients = (jnp.dot(features, d_hidden_one.T, preferred_element_type=jnp.float32), lax.optimization_barrier(jnp.sum(d_hidden_one.astype(jnp.float32), axis=1)), jnp.dot(hidden_one, d_hidden_two.T, preferred_element_type=jnp.float32), lax.optimization_barrier(jnp.sum(d_hidden_two.astype(jnp.float32), axis=1)), jnp.dot(hidden_two, d_logits.T, preferred_element_type=jnp.float32), lax.optimization_barrier(jnp.sum(d_logits.astype(jnp.float32), axis=1)))
    return (coupling, d_features, gradients)

def build_features(desc_line, solid_line, fluid_line):
    cells = solid_line.size
    return jnp.concatenate([desc_line.reshape(desc_line.shape[0], cells), solid_line.reshape(1, cells).astype(jnp.bfloat16), fluid_line.reshape(1, cells).astype(jnp.bfloat16)], axis=0)

def forward_coupling(descriptors, solid, fluid, weights):

    def one_line(line_index):
        desc_line = lax.dynamic_index_in_dim(descriptors, line_index, 1, keepdims=False)
        solid_line = lax.dynamic_index_in_dim(solid, line_index, 0, keepdims=False)
        fluid_line = lax.dynamic_index_in_dim(fluid, line_index, 0, keepdims=False)
        features = build_features(desc_line, solid_line, fluid_line)
        logits = network(features, *weights)[2]
        return coupling_terms(logits)[0].reshape(solid_line.shape)
    return lax.map(one_line, jnp.arange(solid.shape[0], dtype=jnp.int32))

def backward_lines(descriptors, solid, fluid, d_coupling, weights, running):
    w_in, b_in, w_mid, b_mid, w_out, b_out = weights

    def one_line(running, line_index):
        desc_line = lax.dynamic_index_in_dim(descriptors, line_index, 1, keepdims=False)
        solid_line = lax.dynamic_index_in_dim(solid, line_index, 0, keepdims=False)
        fluid_line = lax.dynamic_index_in_dim(fluid, line_index, 0, keepdims=False)
        d_line = lax.dynamic_index_in_dim(d_coupling, line_index, 0, keepdims=False)
        features = build_features(desc_line, solid_line, fluid_line)
        hidden_one, hidden_two, logits = network(features, *weights)
        coupling, d_features, gradients = backprop(features, hidden_one, hidden_two, logits, d_line.reshape(-1), w_in, w_mid, w_out)
        running = tuple((left + right for left, right in zip(running, gradients)))
        line_shape = solid_line.shape
        return (running, (coupling.reshape(line_shape), d_features.reshape((2,) + line_shape)))
    running, (coupling, d_features) = lax.scan(one_line, running, jnp.arange(solid.shape[0], dtype=jnp.int32))
    return (running, coupling, jnp.moveaxis(d_features, 1, 0))

def reference(descriptors, solid_temp, fluid_temp, material, fixed_mask, solid_cond, fluid_cond, w_in, b_in, w_mid, b_mid, w_out, b_out, solid_cot, fluid_cot):
    weights = (w_in, b_in, w_mid, b_mid, w_out, b_out)
    conduct = jnp.stack([material_lookup(material, solid_cond), material_lookup(material, fluid_cond)])
    free_cell = 1.0 - fixed_mask.astype(jnp.float32)
    state = jnp.stack([solid_temp, fluid_temp])
    first_coupling = forward_coupling(descriptors, state[0], state[1], weights)
    coupled = first_coupling * (state[1] - state[0])
    later = state + time_step * free_cell * (conduct * laplace(state) + jnp.stack([coupled, -coupled]))
    running = (jnp.zeros((FEAT, HID), jnp.float32), jnp.zeros((HID,), jnp.float32), jnp.zeros((HID, HID), jnp.float32), jnp.zeros((HID,), jnp.float32), jnp.zeros((HID, 2), jnp.float32), jnp.zeros((2,), jnp.float32))
    cotangent = jnp.stack([solid_cot, fluid_cot])
    for section_state in (later, state):
        upstream = time_step * free_cell * cotangent
        pushed = conduct * upstream
        d_coupling = (section_state[1] - section_state[0]) * (upstream[0] - upstream[1])
        running, coupling, d_features = backward_lines(descriptors, section_state[0], section_state[1], d_coupling, weights, running)
        swing_term = coupling * (upstream[1] - upstream[0])
        cotangent = cotangent + laplace(pushed) + jnp.stack([swing_term, -swing_term]) + d_features
    scale = loss_gain / math.sqrt(NX * NY * NZ)
    return (cotangent[0], cotangent[1], running[0] * scale, running[1] * scale, running[2] * scale, running[3] * scale, running[4] * scale, running[5] * scale)
```

```python
import functools
import math

import jax
import jax.numpy as jnp
from jax import lax
from jax.experimental import pallas as pl
from jax.experimental.pallas import tpu as pltpu
from jax.sharding import PartitionSpec as P

time_step = 0.15
loss_gain = 16.0
DESC, HID, XB, YB = 10, 64, 8, 128
ONES = DESC * XB + 2 * XB
KF = ONES + 16
WIDE = XB * HID
GROUP = 256
STREAMS = 4
BF, F32 = jnp.bfloat16, jnp.float32

VMEM = pl.BlockSpec(memory_space=pltpu.VMEM)
SMEM = pl.BlockSpec(memory_space=pltpu.SMEM)


def nn(a, b):
    return lax.dot_general(a, b, (((1,), (0,)), ((), ())), preferred_element_type=F32)


def nt(a, b):
    return lax.dot_general(a, b, (((1,), (1,)), ((), ())), preferred_element_type=F32)


def tn(a, b):
    return lax.dot_general(a, b, (((0,), (0,)), ((), ())), preferred_element_type=F32)


def lookup(material, table_ref):
    out = jnp.zeros(material.shape, F32)
    for kind in range(4):
        out = jnp.where(material == kind, table_ref[kind], out)
    return out


def iota(shape, dim):
    return lax.broadcasted_iota(jnp.int32, shape, dim)


def pack_columns(fields, depth, lo_ref, hi_ref):
    lane = iota((XB, YB), 1)

    def one(z, carry):
        lo, hi = carry
        for f, field in enumerate(fields):
            v = field(z)
            spot = f * depth + z
            lo = jnp.where(lane == spot, pltpu.roll(v, spot, 1), lo)
            hi = jnp.where(lane == spot, pltpu.roll(v, lax.rem(spot + 1, YB), 1), hi)
        return lo, hi

    zero = jnp.zeros((XB, YB), F32)
    lo, hi = lax.fori_loop(0, depth, one, (zero, zero), unroll=4)
    lo_ref[...] = lo
    hi_ref[...] = hi


def edges_kernel(
    solid, fluid, material, fixed, cond_s, cond_f, cot_s, cot_f,
    row_lo, row_hi, col_lo, col_hi, push,
):
    depth = solid.shape[0]
    weight = time_step * (1.0 - fixed[...].astype(F32))
    kind = material[...]
    push[0] = lookup(kind, cond_s) * (weight * cot_s[...])
    push[1] = lookup(kind, cond_f) * (weight * cot_f[...])
    views = (solid, fluid, push.at[0], push.at[1])
    for f, view in enumerate(views):
        row_lo[f] = view[:, 0, :]
        row_hi[f] = view[:, XB - 1, :]
    pack_columns([lambda z, view=view: view[z] for view in views], depth, col_lo, col_hi)


def spread_weights(w_in, b_in, w_mid, w_out, first_ref, mid_ref, out_ref):
    high = b_in.astype(BF)
    rest = b_in - high.astype(F32)
    middle = rest.astype(BF)
    low = (rest - middle.astype(F32)).astype(BF)
    stacked = jnp.concatenate(
        [w_in.astype(F32), high.astype(F32), middle.astype(F32), low.astype(F32), jnp.zeros((1, HID), F32)],
        axis=0,
    ).astype(BF)
    row, column = iota((16, KF), 0), iota((16, KF), 1)
    for x in range(XB):
        want = jnp.where(row < DESC + 2, row * XB + x, ONES + row - (DESC + 2))
        pick = (column == want).astype(F32).astype(BF)
        first_ref[x * HID : (x + 1) * HID, :] = tn(stacked, pick).astype(BF)
    lane = iota((HID, GROUP), 1)
    spot = iota((HID, GROUP), 0)
    for j in range(GROUP // HID):
        pick = (lane == spot + j * HID).astype(F32).astype(BF)
        if mid_ref is not None:
            mid_ref[0, j * HID : (j + 1) * HID, :] = tn(w_mid, pick).astype(BF)
            mid_ref[1, j * HID : (j + 1) * HID, :] = nn(w_mid, pick).astype(BF)
    spot = iota((HID, WIDE), 0)
    lane = iota((HID, WIDE), 1)
    pick = ((lane - spot) % HID == 0).astype(F32).astype(BF)
    spread = nn(w_out, pick)
    place = (iota((XB, WIDE), 1) // HID) == iota((XB, WIDE), 0)
    for k in range(spread.shape[0]):
        line = jnp.broadcast_to(spread[k : k + 1], (XB, WIDE))
        out_ref[k * XB : (k + 1) * XB, :] = jnp.where(place, line, 0.0).astype(BF)


def features_of(desc, solid, fluid, pair):
    sides = []
    for k in range(2):
        d = desc[:, 2 * pair + k].astype(F32).reshape(DESC * XB, YB)
        sides.append(
            jnp.concatenate([d, solid[k], fluid[k], jnp.ones((16, YB), F32)], axis=0).astype(BF)
        )
    return jnp.concatenate(sides, axis=1)


def blocks(value, size=GROUP):
    return [value[i * size : (i + 1) * size] for i in range(value.shape[0] // size)]


def lockstep(streams):
    alive = list(streams)
    while alive:
        alive = [stream for stream in alive if next(stream, alive) is not alive]


def forward(features, first, mid, out, bias_mid, bias_out):
    tops = [nn(first[g * GROUP : (g + 1) * GROUP], features) for g in range(WIDE // GROUP)]
    yield
    bias = jnp.concatenate([bias_mid[...]] * (GROUP // HID), axis=0)
    bias = jnp.concatenate([bias, bias], axis=1)
    h1, lower = [], []
    for top in tops:
        h1.append(jnp.tanh(top).astype(BF))
        lower.append(nn(mid[0], h1[-1]))
        yield
    h2 = []
    for top in lower:
        h2.append(jnp.tanh(top + bias).astype(BF))
        yield
    h1, h2 = jnp.concatenate(h1, axis=0), jnp.concatenate(h2, axis=0)
    logits = nn(out[...], h2)
    yield
    return h1, h2, logits[:XB] + bias_out[0], logits[XB:] + bias_out[1]


def softplus_terms(v):
    e = jnp.exp(-jnp.abs(v))
    plus = jnp.maximum(v, 0.0) + jnp.log1p(e)
    r = 1.0 / (1.0 + e)
    return plus, jnp.where(v >= 0, r, e * r)


def wide(pair):
    return jnp.concatenate([pair[0], pair[1]], axis=1)


def forward_kernel(
    desc, solid, fluid, w_in, b_in, w_mid, b_mid, w_out, b_out,
    h1_ref, h2_ref, logits_ref, first, mid, out, bias,
):
    spread_weights(w_in[...], b_in[...], w_mid[...], w_out[...], first, mid, out)
    eye = (iota((HID, HID), 0) == iota((HID, HID), 1)).astype(F32)
    column = jnp.sum(eye * b_mid[...], axis=1, keepdims=True)
    bias[...] = jnp.broadcast_to(column, (HID, YB))

    def stream(pair):
        s = [solid[2 * pair + k] for k in range(2)]
        f = [fluid[2 * pair + k] for k in range(2)]
        features = features_of(desc, s, f, pair)
        h1, h2, l0, l1 = yield from forward(features, first, mid, out, bias, b_out)
        h1_ref[pair] = h1
        h2_ref[pair] = h2
        logits_ref[pair, 0] = l0
        logits_ref[pair, 1] = l1

    def one(step, _):
        lockstep([stream(STREAMS * step + k) for k in range(STREAMS)])
        return 0

    lax.fori_loop(0, solid.shape[0] // 2 // STREAMS, one, 0)


def laplace(v, above, below, left, right):
    row, lane = iota((XB, YB), 0), iota((XB, YB), 1)
    down = jnp.where(row == XB - 1, below, pltpu.roll(v, XB - 1, 0))
    up = jnp.where(row == 0, above, pltpu.roll(v, 1, 0))
    east = jnp.where(lane == YB - 1, right, pltpu.roll(v, YB - 1, 1))
    west = jnp.where(lane == 0, left, pltpu.roll(v, 1, 1))
    return down + up + east + west - 4.0 * v


def rim(f, z, depth, rows_lo, rows_hi, cols_lo, cols_hi):
    spot = f * depth + z
    above = jnp.broadcast_to(rows_lo[f, pl.ds(z, 1), :], (XB, YB))
    below = jnp.broadcast_to(rows_hi[f, pl.ds(z, 1), :], (XB, YB))
    left = pltpu.roll(cols_lo[...], lax.rem(YB - spot, YB), 1)
    right = pltpu.roll(cols_hi[...], YB - 1 - spot, 1)
    return above, below, left, right


def backward(features, h1, h2, dl, mid, w_out_t, w_temps):
    tops = [nn(w_out_t[g * GROUP : (g + 1) * GROUP], dl) for g in range(WIDE // GROUP)]
    yield
    dh2, lower = [], []
    for top, h in zip(tops, blocks(h2)):
        h = h.astype(F32)
        dh2.append((top * (1.0 - h * h)).astype(BF))
        lower.append(nn(mid[1], dh2[-1]))
        yield
    dh1 = []
    for top, h in zip(lower, blocks(h1)):
        h = h.astype(F32)
        dh1.append((top * (1.0 - h * h)).astype(BF))
        yield
    dh1, dh2 = jnp.concatenate(dh1, axis=0), jnp.concatenate(dh2, axis=0)
    temps = nn(w_temps[...], dh1)
    one_rows = jnp.ones((16, 2 * YB), BF)
    left = jnp.concatenate(
        [jnp.concatenate([h1[x * HID : (x + 1) * HID], one_rows], axis=0) for x in range(XB)], axis=1
    )
    right = jnp.concatenate([dh2[x * HID : (x + 1) * HID] for x in range(XB)], axis=1)
    terms = nt(features, dh1), nt(left, right), nt(dl, h2)
    yield
    return temps, *terms


def steps_kernel(
    desc, solid, fluid, material, fixed, cond_s, cond_f, cot_s, cot_f, push,
    rows_lo, rows_hi, cols_lo, cols_hi,
    h1_ref, h2_ref, logits_ref, first, mid, out, bias, w_in_temps, b_out,
    part, later_push, row_lo, row_hi, col_lo, col_hi, payload,
    w_out_t, w_temps, acc_in, acc_mid, acc_out, acc_dl,
):
    depth = solid.shape[0]
    eye = (iota((2 * XB, 2 * XB), 0) == iota((2 * XB, 2 * XB), 1)).astype(F32).astype(BF)
    w_out_t[...] = tn(out[...], eye).astype(BF)
    pick = ((iota((HID, WIDE), 1) - iota((HID, WIDE), 0)) % HID == 0).astype(F32).astype(BF)
    spread = nn(w_in_temps[...], pick)
    place = (iota((XB, WIDE), 1) // HID) == iota((XB, WIDE), 0)
    for k in range(2):
        line = jnp.broadcast_to(spread[k : k + 1], (XB, WIDE))
        w_temps[k * XB : (k + 1) * XB, :] = jnp.where(place, line, 0.0).astype(BF)
    acc_in[...] = jnp.zeros_like(acc_in)
    acc_mid[...] = jnp.zeros_like(acc_mid)
    acc_out[...] = jnp.zeros_like(acc_out)
    acc_dl[...] = jnp.zeros_like(acc_dl)

    def stream(pair):
        zs = [2 * pair + k for k in range(2)]
        rims = (rows_lo, rows_hi, cols_lo, cols_hi)
        weight = [time_step * (1.0 - fixed[z].astype(F32)) for z in zs]
        k_s = [lookup(material[z], cond_s) for z in zs]
        k_f = [lookup(material[z], cond_f) for z in zs]
        s0 = [solid[z] for z in zs]
        f0 = [fluid[z] for z in zs]
        h_first, h_slope = softplus_terms(logits_ref[pair, 0])
        a_first, a_slope = softplus_terms(logits_ref[pair, 1])
        c0 = h_first * a_first
        lap_s = [laplace(s0[k], *rim(0, zs[k], depth, *rims)) for k in range(2)]
        lap_f = [laplace(f0[k], *rim(1, zs[k], depth, *rims)) for k in range(2)]
        weight, k_s, k_f = wide(weight), wide(k_s), wide(k_f)
        s0w, f0w = wide(s0), wide(f0)
        gap0 = f0w - s0w
        swing = c0 * gap0
        s1 = s0w + weight * (k_s * wide(lap_s) + swing)
        f1 = f0w + weight * (k_f * wide(lap_f) - swing)

        features1 = features_of(desc, (s1[:, :YB], s1[:, YB:]), (f1[:, :YB], f1[:, YB:]), pair)
        g1, g2, l0, l1 = yield from forward(features1, first, mid, out, bias, b_out)
        h_sf, h_sl = softplus_terms(l0)
        a_sf, a_sl = softplus_terms(l1)
        gs, gf = wide([cot_s[z] for z in zs]), wide([cot_f[z] for z in zs])
        us, uf = weight * gs, weight * gf
        dcoup = (f1 - s1) * (us - uf)
        dl = jnp.concatenate([dcoup * a_sf * h_sl, dcoup * h_sf * a_sl], axis=0).astype(BF)
        temps, t_in, t_mid, t_out = yield from backward(features1, g1, g2, dl, mid, w_out_t, w_temps)
        lap_s = wide([laplace(push[0, z], *rim(2, z, depth, *rims)) for z in zs])
        lap_f = wide([laplace(push[1, z], *rim(3, z, depth, *rims)) for z in zs])
        swing = h_sf * a_sf * (uf - us)
        gs = gs + lap_s + swing + temps[:XB]
        gf = gf + lap_f - swing + temps[XB:]

        us, uf = weight * gs, weight * gf
        ps, pf = k_s * us, k_f * uf
        dcoup = gap0 * (us - uf)
        dl0 = jnp.concatenate([dcoup * a_first * h_slope, dcoup * h_first * a_slope], axis=0).astype(BF)
        features0 = features_of(desc, s0, f0, pair)
        temps, u_in, u_mid, u_out = yield from backward(
            features0, h1_ref[pair], h2_ref[pair], dl0, mid, w_out_t, w_temps
        )
        swing = c0 * (uf - us)
        gs = gs + swing + temps[:XB]
        gf = gf - swing + temps[XB:]
        for k in range(2):
            lanes = slice(k * YB, (k + 1) * YB)
            part[0, zs[k]] = gs[:, lanes]
            part[1, zs[k]] = gf[:, lanes]
            later_push[0, zs[k]] = ps[:, lanes]
            later_push[1, zs[k]] = pf[:, lanes]
        acc_in[...] += t_in + u_in
        acc_mid[...] += t_mid + u_mid
        acc_out[...] += t_out + u_out
        acc_dl[...] += dl.astype(F32) + dl0.astype(F32)

    def one(step, _):
        lockstep([stream(STREAMS * step + k) for k in range(STREAMS)])
        return 0

    lax.fori_loop(0, depth // 2 // STREAMS, one, 0)

    for f in range(2):
        row_lo[f] = later_push[f, :, 0, :]
        row_hi[f] = later_push[f, :, XB - 1, :]
    pack_columns([lambda z, f=f: later_push[f, z] for f in range(2)], depth, col_lo, col_hi)

    def diagonal(acc, blocks):
        same = (iota((XB, WIDE), 1) // HID) == iota((XB, WIDE), 0)
        lines = []
        for b in range(blocks):
            kept = jnp.where(same, acc[b * XB : (b + 1) * XB, :], 0.0)
            lines.append(jnp.sum(kept, axis=0, keepdims=True))
        lines = jnp.concatenate(lines, axis=0)
        total = lines[:, :YB]
        for j in range(1, WIDE // YB):
            total = total + lines[:, j * YB : (j + 1) * YB]
        return total[:, :HID] + total[:, HID:]

    half = HID // 2
    payload[:half, :HID] = acc_mid[:half, :]
    payload[:half, HID:] = acc_mid[half:HID, :]
    payload[half:, :] = jnp.zeros((16, YB), F32)
    payload[half : half + 13, :HID] = diagonal(acc_in, 13)
    payload[half : half + 1, HID:] = acc_mid[HID : HID + 1, :]
    payload[half + 1 : half + 3, HID:] = diagonal(acc_out, 2)
    dl_rows = jnp.sum(acc_dl[...], axis=1, keepdims=True)
    for k in range(2):
        total = jnp.sum(dl_rows[k * XB : (k + 1) * XB], axis=0, keepdims=True)
        payload[half + 3 + k : half + 4 + k, HID:] = jnp.broadcast_to(total, (1, HID))


def finish_kernel(
    scale, part, push, rows_lo, rows_hi, cols_lo, cols_hi, summed,
    adj_s, adj_f, g_w_in, g_b_in, g_w_mid, g_b_mid, g_w_out, g_b_out,
):
    depth = part.shape[1]
    rims = (rows_lo, rows_hi, cols_lo, cols_hi)

    def one(z, _):
        for f, adj in enumerate((adj_s, adj_f)):
            adj[z] = part[f, z] + laplace(push[f, z], *rim(f, z, depth, *rims))
        return 0

    lax.fori_loop(0, depth, one, 0, unroll=4)
    half = HID // 2
    g_w_mid[:half, :] = summed[:half, :HID] * scale
    g_w_mid[half:, :] = summed[:half, HID:] * scale
    g_w_in[...] = summed[half : half + 12, :HID] * scale
    g_b_in[...] = summed[half + 12 : half + 13, :HID] * scale
    g_b_mid[...] = summed[half : half + 1, HID:] * scale
    g_w_out[...] = summed[half + 1 : half + 3, HID:] * scale
    g_b_out[...] = summed[half + 3 : half + 5, HID:] * scale


def shift(value, axis, step):
    count = lax.axis_size(axis)
    pairs = [(i, i + step) for i in range(count) if 0 <= i + step < count]
    return lax.ppermute(value, axis, pairs)


def exchange(row_lo, row_hi, col_lo, col_hi):
    return (
        shift(row_hi, "grp", 1),
        shift(row_lo, "grp", -1),
        shift(col_hi, "col", 1),
        shift(col_lo, "col", -1),
    )


def torus_groups():
    at = lambda x, y, z, core: (2 * z + y % 2) * 32 + 8 * x + 2 * (y // 2) + core
    xs, ys, zs, cores = range(4), range(8), range(8), range(2)
    return (
        [[at(x, y, z, c) for x in xs for c in cores] for y in ys for z in zs],
        [[at(x, y, z, c) for y in ys] for x in xs for z in zs for c in cores],
        [[at(x, y, z, c) for z in zs] for x in xs for y in ys for c in cores],
    )


def total_over_devices(value):
    axes = ("grp", "col")
    count = [lax.axis_size(axis) for axis in axes]
    groups = torus_groups() if count == [16, 32] else ([list(range(count[0] * count[1]))],)
    for members in groups:
        copies = jnp.broadcast_to(value[None], (len(members[0]), *value.shape))
        value = lax.all_to_all(copies, axes, 0, 0, axis_index_groups=members).sum(0)
    return value


def shape(dims, kind=F32):
    return jax.ShapeDtypeStruct(dims, kind)


def shards(
    descriptors, solid_temp, fluid_temp, material, fixed_mask, solid_cond, fluid_cond,
    w_in, b_in, w_mid, b_mid, w_out, b_out, solid_cot, fluid_cot,
):
    depth = solid_temp.shape[0]
    field = (depth, XB, YB)
    rows, column = (4, depth, YB), (XB, YB)
    *edges, push = pl.pallas_call(
        edges_kernel,
        out_shape=[shape(rows), shape(rows), shape(column), shape(column), shape((2,) + field)],
        in_specs=[VMEM] * 4 + [SMEM] * 2 + [VMEM] * 2,
        out_specs=[VMEM] * 5,
        name="edges",
    )(solid_temp, fluid_temp, material, fixed_mask, solid_cond, fluid_cond, solid_cot, fluid_cot)
    received = exchange(*edges)

    pairs = depth // 2
    kept = [
        shape((pairs, WIDE, 2 * YB), BF),
        shape((pairs, WIDE, 2 * YB), BF),
        shape((pairs, 2, XB, 2 * YB)),
        shape((WIDE, KF), BF),
        shape((2, GROUP, GROUP), BF),
        shape((2 * XB, WIDE), BF),
        shape((HID, YB)),
    ]
    saved = pl.pallas_call(
        forward_kernel,
        out_shape=kept,
        in_specs=[VMEM] * 8 + [SMEM],
        out_specs=[VMEM] * len(kept),
        cost_estimate=pl.CostEstimate(flops=2**29, bytes_accessed=2**24, transcendentals=2**22),
        name="forward",
    )(descriptors, solid_temp, fluid_temp, w_in, b_in[None], w_mid, b_mid[None], w_out.T, b_out)

    part, later_push, *edges, payload = pl.pallas_call(
        steps_kernel,
        out_shape=[
            shape((2,) + field),
            shape((2,) + field),
            shape((2, depth, YB)),
            shape((2, depth, YB)),
            shape(column),
            shape(column),
            shape((48, YB)),
        ],
        in_specs=[VMEM] * 5 + [SMEM] * 2 + [VMEM] * 15 + [SMEM],
        out_specs=[VMEM] * 7,
        scratch_shapes=[
            pltpu.VMEM((WIDE, 2 * XB), BF),
            pltpu.VMEM((2 * XB, WIDE), BF),
            pltpu.VMEM((KF, WIDE), F32),
            pltpu.VMEM((HID + 16, HID), F32),
            pltpu.VMEM((2 * XB, WIDE), F32),
            pltpu.VMEM((2 * XB, 2 * YB), F32),
        ],
        cost_estimate=pl.CostEstimate(flops=2**31, bytes_accessed=2**24, transcendentals=2**22),
        name="steps",
    )(
        descriptors, solid_temp, fluid_temp, material, fixed_mask, solid_cond, fluid_cond,
        solid_cot, fluid_cot, push, *received, *saved, w_in[DESC:], b_out,
    )
    received = exchange(*edges)
    summed = total_over_devices(payload)

    cells = solid_temp.size * lax.axis_size("grp") * lax.axis_size("col")
    scale = loss_gain / math.sqrt(cells)
    adj_s, adj_f, *grads = pl.pallas_call(
        functools.partial(finish_kernel, scale),
        out_shape=[
            shape(field), shape(field),
            shape((12, HID)), shape((1, HID)), shape((HID, HID)), shape((1, HID)),
            shape((2, HID)), shape((2, HID)),
        ],
        in_specs=[VMEM] * 7,
        out_specs=[VMEM] * 8,
        name="finish",
    )(part, later_push, *received, summed)
    return (
        adj_s, adj_f, grads[0], grads[1][0], grads[2], grads[3][0], grads[4].T, grads[5][:, 0],
    )


def solution(mesh):
    field, whole = P(None, "grp", "col"), P()
    placed = (
        (P(None, None, "grp", "col"),) + (field,) * 4 + (whole,) * 8 + (field,) * 2
    )
    return jax.shard_map(
        shards,
        mesh=mesh,
        in_specs=placed,
        out_specs=(field, field) + (whole,) * 6,
        check_vma=False,
    )
```

```python
import functools
import math

import jax
import jax.numpy as jnp
from jax import lax
from jax.experimental import pallas as pl
from jax.experimental.pallas import tpu as pltpu
from jax.sharding import PartitionSpec as P

time_step = 0.15
loss_gain = 16.0
LOADED = 12
DESC, HID, XB, YB = 10, 64, 8, 128
ONES = DESC * XB + 2 * XB
KF = ONES + 16
WIDE = XB * HID
GROUP = 256
STREAMS = 8
BF, F32 = jnp.bfloat16, jnp.float32

VMEM = pl.BlockSpec(memory_space=pltpu.VMEM)
SMEM = pl.BlockSpec(memory_space=pltpu.SMEM)
HBM = pl.BlockSpec(memory_space=pltpu.HBM)


def nn(a, b):
    return lax.dot_general(a, b, (((1,), (0,)), ((), ())), preferred_element_type=F32)


def nt(a, b):
    return lax.dot_general(a, b, (((1,), (1,)), ((), ())), preferred_element_type=F32)


def tn(a, b):
    return lax.dot_general(a, b, (((0,), (0,)), ((), ())), preferred_element_type=F32)


def lookup(material, table_ref):
    out = jnp.zeros(material.shape, F32)
    for kind in range(4):
        out = jnp.where(material == kind, table_ref[kind], out)
    return out


def iota(shape, dim):
    return lax.broadcasted_iota(jnp.int32, shape, dim)


def pack_columns(fields, depth, lo_ref, hi_ref):
    lane = iota((XB, YB), 1)

    def one(z, carry):
        lo, hi = carry
        for f, field in enumerate(fields):
            v = field(z)
            spot = f * depth + z
            lo = jnp.where(lane == spot, pltpu.roll(v, spot, 1), lo)
            hi = jnp.where(lane == spot, pltpu.roll(v, lax.rem(spot + 1, YB), 1), hi)
        return lo, hi

    zero = jnp.zeros((XB, YB), F32)
    lo, hi = lax.fori_loop(0, depth, one, (zero, zero), unroll=4)
    lo_ref[...] = lo
    hi_ref[...] = hi


def edges_kernel(cond_s, cond_f, *refs):
    far, near, sems = refs[:LOADED], refs[LOADED : 2 * LOADED], refs[-1]
    row_lo, row_hi, col_lo, col_hi, push = refs[2 * LOADED : -1]
    copies = [pltpu.make_async_copy(far[i], near[i], sems.at[i]) for i in range(LOADED)]
    for copy in copies:
        copy.start()
    for copy in copies[:6]:
        copy.wait()
    solid, fluid, material, fixed, cot_s, cot_f = near[:6]
    depth = solid.shape[0]
    weight = time_step * (1.0 - fixed[...].astype(F32))
    kind = material[...]
    push[0] = lookup(kind, cond_s) * (weight * cot_s[...])
    push[1] = lookup(kind, cond_f) * (weight * cot_f[...])
    views = (solid, fluid, push.at[0], push.at[1])
    for f, view in enumerate(views):
        row_lo[f] = view[:, 0, :]
        row_hi[f] = view[:, XB - 1, :]
    pack_columns([lambda z, view=view: view[z] for view in views], depth, col_lo, col_hi)
    for copy in copies[6:]:
        copy.wait()


def spread_weights(w_in, b_in, w_mid, w_out, first_ref, mid_ref, out_ref):
    high = b_in.astype(BF)
    rest = b_in - high.astype(F32)
    middle = rest.astype(BF)
    low = (rest - middle.astype(F32)).astype(BF)
    stacked = jnp.concatenate(
        [w_in.astype(F32), high.astype(F32), middle.astype(F32), low.astype(F32), jnp.zeros((1, HID), F32)],
        axis=0,
    ).astype(BF)
    row, column = iota((16, KF), 0), iota((16, KF), 1)
    for x in range(XB):
        want = jnp.where(row < DESC + 2, row * XB + x, ONES + row - (DESC + 2))
        pick = (column == want).astype(F32).astype(BF)
        first_ref[x * HID : (x + 1) * HID, :] = tn(stacked, pick).astype(BF)
    lane = iota((HID, GROUP), 1)
    spot = iota((HID, GROUP), 0)
    for j in range(GROUP // HID):
        pick = (lane == spot + j * HID).astype(F32).astype(BF)
        if mid_ref is not None:
            mid_ref[0, j * HID : (j + 1) * HID, :] = tn(w_mid, pick).astype(BF)
            mid_ref[1, j * HID : (j + 1) * HID, :] = nn(w_mid, pick).astype(BF)
    spot = iota((HID, WIDE), 0)
    lane = iota((HID, WIDE), 1)
    pick = ((lane - spot) % HID == 0).astype(F32).astype(BF)
    spread = nn(w_out, pick)
    place = (iota((XB, WIDE), 1) // HID) == iota((XB, WIDE), 0)
    for k in range(spread.shape[0]):
        line = jnp.broadcast_to(spread[k : k + 1], (XB, WIDE))
        out_ref[k * XB : (k + 1) * XB, :] = jnp.where(place, line, 0.0).astype(BF)


def features_of(desc, solid, fluid, pair):
    sides = []
    for k in range(2):
        d = desc[:, 2 * pair + k].astype(F32).reshape(DESC * XB, YB)
        sides.append(
            jnp.concatenate([d, solid[k], fluid[k], jnp.ones((16, YB), F32)], axis=0).astype(BF)
        )
    return jnp.concatenate(sides, axis=1)


def blocks(value, size=GROUP):
    return [value[i * size : (i + 1) * size] for i in range(value.shape[0] // size)]


def lockstep(streams):
    alive = list(streams)
    while alive:
        alive = [stream for stream in alive if next(stream, alive) is not alive]


def forward(features, first, mid, out, bias_mid, bias_out):
    tops = [nn(first[g * GROUP : (g + 1) * GROUP], features) for g in range(WIDE // GROUP)]
    yield
    bias = jnp.concatenate([bias_mid[...]] * (GROUP // HID), axis=0)
    bias = jnp.concatenate([bias, bias], axis=1)
    h1, lower = [], []
    for top in tops:
        h1.append(jnp.tanh(top).astype(BF))
        lower.append(nn(mid[0], h1[-1]))
        yield
    h2 = []
    for top in lower:
        h2.append(jnp.tanh(top + bias).astype(BF))
        yield
    h1, h2 = jnp.concatenate(h1, axis=0), jnp.concatenate(h2, axis=0)
    logits = nn(out[...], h2)
    yield
    return h1, h2, logits[:XB] + bias_out[0], logits[XB:] + bias_out[1]


def softplus_terms(v):
    e = jnp.exp(-jnp.abs(v))
    plus = jnp.maximum(v, 0.0) + jnp.log1p(e)
    r = 1.0 / (1.0 + e)
    return plus, jnp.where(v >= 0, r, e * r)


def wide(pair):
    return jnp.concatenate([pair[0], pair[1]], axis=1)


def forward_kernel(
    desc, solid, fluid, w_in, b_in, w_mid, b_mid, w_out, b_out,
    h1_ref, h2_ref, logits_ref, first, mid, out, bias,
):
    spread_weights(w_in[...], b_in[...], w_mid[...], w_out[...], first, mid, out)
    eye = (iota((HID, HID), 0) == iota((HID, HID), 1)).astype(F32)
    column = jnp.sum(eye * b_mid[...], axis=1, keepdims=True)
    bias[...] = jnp.broadcast_to(column, (HID, YB))

    def stream(pair):
        s = [solid[2 * pair + k] for k in range(2)]
        f = [fluid[2 * pair + k] for k in range(2)]
        features = features_of(desc, s, f, pair)
        h1, h2, l0, l1 = yield from forward(features, first, mid, out, bias, b_out)
        h1_ref[pair] = h1
        h2_ref[pair] = h2
        logits_ref[pair, 0] = l0
        logits_ref[pair, 1] = l1

    def one(step, _):
        lockstep([stream(STREAMS * step + k) for k in range(STREAMS)])
        return 0

    lax.fori_loop(0, solid.shape[0] // 2 // STREAMS, one, 0)


def laplace(v, above, below, left, right):
    row, lane = iota((XB, YB), 0), iota((XB, YB), 1)
    down = jnp.where(row == XB - 1, below, pltpu.roll(v, XB - 1, 0))
    up = jnp.where(row == 0, above, pltpu.roll(v, 1, 0))
    east = jnp.where(lane == YB - 1, right, pltpu.roll(v, YB - 1, 1))
    west = jnp.where(lane == 0, left, pltpu.roll(v, 1, 1))
    return down + up + east + west - 4.0 * v


def rim(f, z, depth, rows_lo, rows_hi, cols_lo, cols_hi):
    spot = f * depth + z
    above = jnp.broadcast_to(rows_lo[f, pl.ds(z, 1), :], (XB, YB))
    below = jnp.broadcast_to(rows_hi[f, pl.ds(z, 1), :], (XB, YB))
    left = pltpu.roll(cols_lo[...], lax.rem(YB - spot, YB), 1)
    right = pltpu.roll(cols_hi[...], YB - 1 - spot, 1)
    return above, below, left, right


def backward(features, h1, h2, dl, mid, w_out_t, w_temps):
    tops = [nn(w_out_t[g * GROUP : (g + 1) * GROUP], dl) for g in range(WIDE // GROUP)]
    yield
    dh2, lower = [], []
    for top, h in zip(tops, blocks(h2)):
        h = h.astype(F32)
        dh2.append((top * (1.0 - h * h)).astype(BF))
        lower.append(nn(mid[1], dh2[-1]))
        yield
    dh1 = []
    for top, h in zip(lower, blocks(h1)):
        h = h.astype(F32)
        dh1.append((top * (1.0 - h * h)).astype(BF))
        yield
    dh1, dh2 = jnp.concatenate(dh1, axis=0), jnp.concatenate(dh2, axis=0)
    temps = nn(w_temps[...], dh1)
    one_rows = jnp.ones((16, 2 * YB), BF)
    left = jnp.concatenate(
        [jnp.concatenate([h1[x * HID : (x + 1) * HID], one_rows], axis=0) for x in range(XB)], axis=1
    )
    right = jnp.concatenate([dh2[x * HID : (x + 1) * HID] for x in range(XB)], axis=1)
    terms = nt(features, dh1), nt(left, right), nt(dl, h2)
    yield
    return temps, *terms


def steps_kernel(
    desc, solid, fluid, material, fixed, cond_s, cond_f, cot_s, cot_f, push,
    rows_lo, rows_hi, cols_lo, cols_hi,
    h1_ref, h2_ref, logits_ref, first, mid, out, bias, w_in, b_out,
    part, later_push, row_lo, row_hi, col_lo, col_hi, payload,
    w_out_t, w_temps, acc_in, acc_mid, acc_out, acc_dl,
):
    depth = solid.shape[0]
    eye = (iota((2 * XB, 2 * XB), 0) == iota((2 * XB, 2 * XB), 1)).astype(F32).astype(BF)
    w_out_t[...] = tn(out[...], eye).astype(BF)
    pick = ((iota((HID, WIDE), 1) - iota((HID, WIDE), 0)) % HID == 0).astype(F32).astype(BF)
    spread = nn(w_in[...].astype(F32)[DESC:].astype(BF), pick)
    place = (iota((XB, WIDE), 1) // HID) == iota((XB, WIDE), 0)
    for k in range(2):
        line = jnp.broadcast_to(spread[k : k + 1], (XB, WIDE))
        w_temps[k * XB : (k + 1) * XB, :] = jnp.where(place, line, 0.0).astype(BF)
    acc_in[...] = jnp.zeros_like(acc_in)
    acc_mid[...] = jnp.zeros_like(acc_mid)
    acc_out[...] = jnp.zeros_like(acc_out)
    acc_dl[...] = jnp.zeros_like(acc_dl)

    def stream(pair):
        zs = [2 * pair + k for k in range(2)]
        rims = (rows_lo, rows_hi, cols_lo, cols_hi)
        weight = [time_step * (1.0 - fixed[z].astype(F32)) for z in zs]
        k_s = [lookup(material[z], cond_s) for z in zs]
        k_f = [lookup(material[z], cond_f) for z in zs]
        s0 = [solid[z] for z in zs]
        f0 = [fluid[z] for z in zs]
        h_first, h_slope = softplus_terms(logits_ref[pair, 0])
        a_first, a_slope = softplus_terms(logits_ref[pair, 1])
        c0 = h_first * a_first
        lap_s = [laplace(s0[k], *rim(0, zs[k], depth, *rims)) for k in range(2)]
        lap_f = [laplace(f0[k], *rim(1, zs[k], depth, *rims)) for k in range(2)]
        weight, k_s, k_f = wide(weight), wide(k_s), wide(k_f)
        s0w, f0w = wide(s0), wide(f0)
        gap0 = f0w - s0w
        swing = c0 * gap0
        s1 = s0w + weight * (k_s * wide(lap_s) + swing)
        f1 = f0w + weight * (k_f * wide(lap_f) - swing)

        features1 = features_of(desc, (s1[:, :YB], s1[:, YB:]), (f1[:, :YB], f1[:, YB:]), pair)
        g1, g2, l0, l1 = yield from forward(features1, first, mid, out, bias, b_out)
        h_sf, h_sl = softplus_terms(l0)
        a_sf, a_sl = softplus_terms(l1)
        gs, gf = wide([cot_s[z] for z in zs]), wide([cot_f[z] for z in zs])
        us, uf = weight * gs, weight * gf
        dcoup = (f1 - s1) * (us - uf)
        dl = jnp.concatenate([dcoup * a_sf * h_sl, dcoup * h_sf * a_sl], axis=0).astype(BF)
        temps, t_in, t_mid, t_out = yield from backward(features1, g1, g2, dl, mid, w_out_t, w_temps)
        lap_s = wide([laplace(push[0, z], *rim(2, z, depth, *rims)) for z in zs])
        lap_f = wide([laplace(push[1, z], *rim(3, z, depth, *rims)) for z in zs])
        swing = h_sf * a_sf * (uf - us)
        gs = gs + lap_s + swing + temps[:XB]
        gf = gf + lap_f - swing + temps[XB:]

        us, uf = weight * gs, weight * gf
        ps, pf = k_s * us, k_f * uf
        dcoup = gap0 * (us - uf)
        dl0 = jnp.concatenate([dcoup * a_first * h_slope, dcoup * h_first * a_slope], axis=0).astype(BF)
        features0 = features_of(desc, s0, f0, pair)
        temps, u_in, u_mid, u_out = yield from backward(
            features0, h1_ref[pair], h2_ref[pair], dl0, mid, w_out_t, w_temps
        )
        swing = c0 * (uf - us)
        gs = gs + swing + temps[:XB]
        gf = gf - swing + temps[XB:]
        for k in range(2):
            lanes = slice(k * YB, (k + 1) * YB)
            part[0, zs[k]] = gs[:, lanes]
            part[1, zs[k]] = gf[:, lanes]
            later_push[0, zs[k]] = ps[:, lanes]
            later_push[1, zs[k]] = pf[:, lanes]
        acc_in[...] += t_in + u_in
        acc_mid[...] += t_mid + u_mid
        acc_out[...] += t_out + u_out
        acc_dl[...] += dl.astype(F32) + dl0.astype(F32)

    def one(step, _):
        lockstep([stream(STREAMS * step + k) for k in range(STREAMS)])
        return 0

    lax.fori_loop(0, depth // 2 // STREAMS, one, 0)

    for f in range(2):
        row_lo[f] = later_push[f, :, 0, :]
        row_hi[f] = later_push[f, :, XB - 1, :]
    pack_columns([lambda z, f=f: later_push[f, z] for f in range(2)], depth, col_lo, col_hi)

    def diagonal(acc, blocks):
        same = (iota((XB, WIDE), 1) // HID) == iota((XB, WIDE), 0)
        lines = []
        for b in range(blocks):
            kept = jnp.where(same, acc[b * XB : (b + 1) * XB, :], 0.0)
            lines.append(jnp.sum(kept, axis=0, keepdims=True))
        lines = jnp.concatenate(lines, axis=0)
        total = lines[:, :YB]
        for j in range(1, WIDE // YB):
            total = total + lines[:, j * YB : (j + 1) * YB]
        return total[:, :HID] + total[:, HID:]

    half = HID // 2
    grads = payload.at[0]
    grads[:half, :HID] = acc_mid[:half, :]
    grads[:half, HID:] = acc_mid[half:HID, :]
    grads[half:, :] = jnp.zeros((16, YB), F32)
    grads[half : half + 13, :HID] = diagonal(acc_in, 13)
    grads[half : half + 1, HID:] = acc_mid[HID : HID + 1, :]
    grads[half + 1 : half + 3, HID:] = diagonal(acc_out, 2)
    dl_rows = jnp.sum(acc_dl[...], axis=1, keepdims=True)
    for k in range(2):
        total = jnp.sum(dl_rows[k * XB : (k + 1) * XB], axis=0, keepdims=True)
        grads[half + 3 + k : half + 4 + k, HID:] = jnp.broadcast_to(total, (1, HID))
    for copy in range(1, payload.shape[0]):
        payload[copy] = payload[0]


def finish_kernel(
    scale, part, push, rows_lo, rows_hi, cols_lo, cols_hi, summed,
    adj_s, adj_f, g_w_in, g_b_in, g_w_mid, g_b_mid, g_w_out, g_b_out,
):
    depth = part.shape[1]
    rims = (rows_lo, rows_hi, cols_lo, cols_hi)

    def one(z, _):
        for f, adj in enumerate((adj_s, adj_f)):
            adj[z] = part[f, z] + laplace(push[f, z], *rim(f, z, depth, *rims))
        return 0

    lax.fori_loop(0, depth, one, 0, unroll=4)
    half = HID // 2
    g_w_mid[:half, :] = summed[:half, :HID] * scale
    g_w_mid[half:, :] = summed[:half, HID:] * scale
    g_w_in[...] = summed[half : half + 12, :HID] * scale
    g_b_in[...] = summed[half + 12 : half + 13, :HID] * scale
    g_b_mid[...] = summed[half : half + 1, HID:] * scale
    g_w_out[...] = summed[half + 1 : half + 3, HID:] * scale
    first = iota((1, HID), 1) == 0
    for k in range(2):
        g_b_out[k] = jnp.sum(jnp.where(first, summed[half + 3 + k : half + 4 + k, HID:], 0.0)) * scale


def shift(value, axis, step):
    count = lax.axis_size(axis)
    pairs = [(i, i + step) for i in range(count) if 0 <= i + step < count]
    return lax.ppermute(value, axis, pairs)


def exchange(row_lo, row_hi, col_lo, col_hi):
    return (
        shift(row_hi, "grp", 1),
        shift(row_lo, "grp", -1),
        shift(col_hi, "col", 1),
        shift(col_lo, "col", -1),
    )


def torus_groups():
    at = lambda x, y, z, core: (2 * z + y % 2) * 32 + 8 * x + 2 * (y // 2) + core
    xs, ys, zs, cores = range(4), range(8), range(8), range(2)
    return (
        [[at(x, y, z, c) for x in xs for c in cores] for y in ys for z in zs],
        [[at(x, y, z, c) for y in ys] for x in xs for z in zs for c in cores],
        [[at(x, y, z, c) for z in zs] for x in xs for y in ys for c in cores],
    )


def rings():
    count = lax.axis_size("grp"), lax.axis_size("col")
    return torus_groups() if count == (16, 32) else ([list(range(count[0] * count[1]))],)


def total_over_devices(copies):
    axes = ("grp", "col")
    for members in rings():
        if copies.ndim == 2:
            copies = jnp.broadcast_to(copies[None], (len(members[0]), *copies.shape))
        copies = lax.all_to_all(copies, axes, 0, 0, axis_index_groups=members).sum(0)
    return copies


def shape(dims, kind=F32):
    return jax.ShapeDtypeStruct(dims, kind)


def shards(
    descriptors, solid_temp, fluid_temp, material, fixed_mask, solid_cond, fluid_cond,
    w_in, b_in, w_mid, b_mid, w_out, b_out, solid_cot, fluid_cot,
):
    depth = solid_temp.shape[0]
    field = (depth, XB, YB)
    rows, column = (4, depth, YB), (XB, YB)
    given = (
        solid_temp, fluid_temp, material, fixed_mask, solid_cot, fluid_cot,
        descriptors, w_in, b_in[None], w_mid, b_mid[None], w_out.T,
    )
    *loaded, row_lo, row_hi, col_lo, col_hi, push = pl.pallas_call(
        edges_kernel,
        out_shape=[pltpu.VMEM(v.shape, v.dtype) for v in given]
        + [shape(rows), shape(rows), shape(column), shape(column), pltpu.VMEM((2,) + field, F32)],
        in_specs=[SMEM] * 2 + [HBM] * LOADED,
        out_specs=[VMEM] * (LOADED + 5),
        scratch_shapes=[pltpu.SemaphoreType.DMA((LOADED,))],
        compiler_params=pltpu.CompilerParams(vmem_limit_bytes=65_050_000),
        name="edges",
    )(solid_cond, fluid_cond, *given)
    edges = row_lo, row_hi, col_lo, col_hi
    solid, fluid, material, fixed, cot_s, cot_f, desc, *weights = loaded
    received = exchange(*edges)

    pairs = depth // 2
    kept = [
        pltpu.VMEM((pairs, WIDE, 2 * YB), BF),
        pltpu.VMEM((pairs, WIDE, 2 * YB), BF),
        pltpu.VMEM((pairs, 2, XB, 2 * YB), F32),
        pltpu.VMEM((WIDE, KF), BF),
        pltpu.VMEM((2, GROUP, GROUP), BF),
        pltpu.VMEM((2 * XB, WIDE), BF),
        pltpu.VMEM((HID, YB), F32),
    ]
    saved = pl.pallas_call(
        forward_kernel,
        out_shape=kept,
        in_specs=[VMEM] * 8 + [SMEM],
        out_specs=[VMEM] * len(kept),
        cost_estimate=pl.CostEstimate(flops=2**29, bytes_accessed=2**24, transcendentals=2**22),
        name="forward",
        compiler_params=pltpu.CompilerParams(vmem_limit_bytes=24 * 2**20),
    )(desc, solid, fluid, *weights, b_out)

    part, later_push, *edges, payload = pl.pallas_call(
        steps_kernel,
        out_shape=[
            shape((2,) + field),
            shape((2,) + field),
            shape((2, depth, YB)),
            shape((2, depth, YB)),
            shape(column),
            shape(column),
            shape((len(rings()[0][0]), 48, YB)),
        ],
        in_specs=[VMEM] * 5 + [SMEM] * 2 + [VMEM] * 15 + [SMEM],
        out_specs=[VMEM] * 7,
        scratch_shapes=[
            pltpu.VMEM((WIDE, 2 * XB), BF),
            pltpu.VMEM((2 * XB, WIDE), BF),
            pltpu.VMEM((KF, WIDE), F32),
            pltpu.VMEM((HID + 16, HID), F32),
            pltpu.VMEM((2 * XB, WIDE), F32),
            pltpu.VMEM((2 * XB, 2 * YB), F32),
        ],
        cost_estimate=pl.CostEstimate(flops=2**31, bytes_accessed=2**24, transcendentals=2**22),
        name="steps",
        compiler_params=pltpu.CompilerParams(vmem_limit_bytes=32 * 2**20),
    )(
        desc, solid, fluid, material, fixed, solid_cond, fluid_cond,
        cot_s, cot_f, push, *received, *saved, weights[0], b_out,
    )
    received = exchange(*edges)
    summed = total_over_devices(payload)

    cells = solid_temp.size * lax.axis_size("grp") * lax.axis_size("col")
    scale = loss_gain / math.sqrt(cells)
    adj_s, adj_f, *grads = pl.pallas_call(
        functools.partial(finish_kernel, scale),
        out_shape=[
            shape(field), shape(field),
            shape((12, HID)), shape((1, HID)), shape((HID, HID)), shape((1, HID)),
            shape((2, HID)), shape((2,)),
        ],
        in_specs=[VMEM] * 7,
        out_specs=[VMEM] * 7 + [SMEM],
        name="finish",
        compiler_params=pltpu.CompilerParams(vmem_limit_bytes=16 * 2**20),
    )(part, later_push, *received, summed)
    return (
        adj_s, adj_f, grads[0], grads[1][0], grads[2], grads[3][0], grads[4].T, grads[5],
    )


def solution(mesh):
    field, whole = P(None, "grp", "col"), P()
    placed = (
        (P(None, None, "grp", "col"),) + (field,) * 4 + (whole,) * 8 + (field,) * 2
    )
    return jax.shard_map(
        shards,
        mesh=mesh,
        in_specs=placed,
        out_specs=(field, field) + (whole,) * 6,
        check_vma=False,
    )
```

```python
import functools
import math

import jax
import jax.numpy as jnp
from jax import lax
from jax.experimental import pallas as pl
from jax.experimental.pallas import tpu as pltpu
from jax.sharding import PartitionSpec as P

time_step = 0.15
loss_gain = 16.0
LOADED = 13
DESC, HID, XB, YB = 10, 64, 8, 128
ONES = DESC * XB + 2 * XB
KF = ONES + 16
WIDE = XB * HID
GROUP = 256
STREAMS = 8
BF, F32 = jnp.bfloat16, jnp.float32

VMEM = pl.BlockSpec(memory_space=pltpu.VMEM)
SMEM = pl.BlockSpec(memory_space=pltpu.SMEM)
HBM = pl.BlockSpec(memory_space=pltpu.HBM)


def nn(a, b):
    return lax.dot_general(a, b, (((1,), (0,)), ((), ())), preferred_element_type=F32)


def nt(a, b):
    return lax.dot_general(a, b, (((1,), (1,)), ((), ())), preferred_element_type=F32)


def tn(a, b):
    return lax.dot_general(a, b, (((0,), (0,)), ((), ())), preferred_element_type=F32)


def lookup(material, table_ref):
    out = jnp.zeros(material.shape, F32)
    for kind in range(4):
        out = jnp.where(material == kind, table_ref[kind], out)
    return out


def iota(shape, dim):
    return lax.broadcasted_iota(jnp.int32, shape, dim)


def pack_columns(fields, depth, lo_ref, hi_ref):
    lane = iota((XB, YB), 1)

    def one(z, carry):
        lo, hi = carry
        for f, field in enumerate(fields):
            v = field(z)
            spot = f * depth + z
            lo = jnp.where(lane == spot, pltpu.roll(v, spot, 1), lo)
            hi = jnp.where(lane == spot, pltpu.roll(v, (spot + 1) % YB, 1), hi)
        return lo, hi

    zero = jnp.zeros((XB, YB), F32)
    lo, hi = zero, zero
    for z in range(depth):
        lo, hi = one(z, (lo, hi))
    lo_ref[...] = lo
    hi_ref[...] = hi


def edges_kernel(cond_s, cond_f, *refs):
    far, near, sems = refs[:LOADED], refs[LOADED : 2 * LOADED], refs[-1]
    row_lo, row_hi, col_lo, col_hi, push = refs[2 * LOADED : -1]
    copies = [pltpu.make_async_copy(far[i], near[i], sems.at[i]) for i in range(LOADED)]
    for copy in copies:
        copy.start()
    for copy in copies[:6]:
        copy.wait()
    solid, fluid, material, fixed, cot_s, cot_f = near[:6]
    depth = solid.shape[0]
    weight = time_step * (1.0 - fixed[...].astype(F32))
    kind = material[...]
    push[0] = lookup(kind, cond_s) * (weight * cot_s[...])
    push[1] = lookup(kind, cond_f) * (weight * cot_f[...])
    views = (solid, fluid, push.at[0], push.at[1])
    for f, view in enumerate(views):
        row_lo[f] = view[:, 0, :]
        row_hi[f] = view[:, XB - 1, :]
    pack_columns([lambda z, view=view: view[z] for view in views], depth, col_lo, col_hi)
    for copy in copies[6:]:
        copy.wait()


def spread_weights(w_in, b_in, w_mid, w_out, first_ref, mid_ref, out_ref):
    high = b_in.astype(BF)
    rest = b_in - high.astype(F32)
    middle = rest.astype(BF)
    low = (rest - middle.astype(F32)).astype(BF)
    stacked = jnp.concatenate(
        [w_in.astype(F32), high.astype(F32), middle.astype(F32), low.astype(F32), jnp.zeros((1, HID), F32)],
        axis=0,
    ).astype(BF)
    row, column = iota((16, KF), 0), iota((16, KF), 1)
    for x in range(XB):
        want = jnp.where(row < DESC + 2, row * XB + x, ONES + row - (DESC + 2))
        pick = (column == want).astype(F32).astype(BF)
        first_ref[x * HID : (x + 1) * HID, :] = tn(stacked, pick).astype(BF)
    lane = iota((HID, GROUP), 1)
    spot = iota((HID, GROUP), 0)
    for j in range(GROUP // HID):
        pick = (lane == spot + j * HID).astype(F32).astype(BF)
        if mid_ref is not None:
            mid_ref[0, j * HID : (j + 1) * HID, :] = tn(w_mid, pick).astype(BF)
            mid_ref[1, j * HID : (j + 1) * HID, :] = nn(w_mid, pick).astype(BF)
    spot = iota((HID, WIDE), 0)
    lane = iota((HID, WIDE), 1)
    pick = ((lane - spot) % HID == 0).astype(F32).astype(BF)
    spread = nn(w_out, pick)
    place = (iota((XB, WIDE), 1) // HID) == iota((XB, WIDE), 0)
    for k in range(spread.shape[0]):
        line = jnp.broadcast_to(spread[k : k + 1], (XB, WIDE))
        out_ref[k * XB : (k + 1) * XB, :] = jnp.where(place, line, 0.0).astype(BF)


def features_of(desc, solid, fluid, pair):
    sides = []
    for k in range(2):
        d = desc[:, 2 * pair + k].astype(F32).reshape(DESC * XB, YB)
        sides.append(
            jnp.concatenate([d, solid[k], fluid[k], jnp.ones((16, YB), F32)], axis=0).astype(BF)
        )
    return jnp.concatenate(sides, axis=1)


def blocks(value, size=GROUP):
    return [value[i * size : (i + 1) * size] for i in range(value.shape[0] // size)]


def lockstep(streams):
    alive = list(streams)
    while alive:
        alive = [stream for stream in alive if next(stream, alive) is not alive]


def forward(features, first, mid, out, bias_mid, bias_out):
    tops = [nn(first[g * GROUP : (g + 1) * GROUP], features) for g in range(WIDE // GROUP)]
    yield
    bias = jnp.concatenate([bias_mid[...]] * (GROUP // HID), axis=0)
    bias = jnp.concatenate([bias, bias], axis=1)
    h1, lower = [], []
    for top in tops:
        h1.append(jnp.tanh(top).astype(BF))
        lower.append(nn(mid[0], h1[-1]))
        yield
    h2 = []
    for top in lower:
        h2.append(jnp.tanh(top + bias).astype(BF))
        yield
    h1, h2 = jnp.concatenate(h1, axis=0), jnp.concatenate(h2, axis=0)
    logits = nn(out[...], h2)
    yield
    return h1, h2, logits[:XB] + bias_out[:, :1], logits[XB:] + bias_out[:, 1:]


def softplus_terms(v):
    e = jnp.exp(-jnp.abs(v))
    plus = jnp.maximum(v, 0.0) + jnp.log1p(e)
    r = 1.0 / (1.0 + e)
    return plus, jnp.where(v >= 0, r, e * r)


def wide(pair):
    return jnp.concatenate([pair[0], pair[1]], axis=1)


def forward_kernel(
    desc, solid, fluid, w_in, b_in, w_mid, b_mid, w_out, b_out,
    h1_ref, h2_ref, logits_ref, first, mid, out, bias,
):
    spread_weights(w_in[...], b_in[...], w_mid[...], w_out[...], first, mid, out)
    eye = (iota((HID, HID), 0) == iota((HID, HID), 1)).astype(F32)
    column = jnp.sum(eye * b_mid[...], axis=1, keepdims=True)
    bias[...] = jnp.broadcast_to(column, (HID, YB))

    def stream(pair):
        s = [solid[2 * pair + k] for k in range(2)]
        f = [fluid[2 * pair + k] for k in range(2)]
        features = features_of(desc, s, f, pair)
        h1, h2, l0, l1 = yield from forward(features, first, mid, out, bias, b_out)
        h1_ref[pair] = h1
        h2_ref[pair] = h2
        logits_ref[pair, 0] = l0
        logits_ref[pair, 1] = l1

    def one(step, _):
        lockstep([stream(STREAMS * step + k) for k in range(STREAMS)])
        return 0

    lax.fori_loop(0, solid.shape[0] // 2 // STREAMS, one, 0)


def laplace(v, above, below, left, right):
    row, lane = iota((XB, YB), 0), iota((XB, YB), 1)
    down = jnp.where(row == XB - 1, below, pltpu.roll(v, XB - 1, 0))
    up = jnp.where(row == 0, above, pltpu.roll(v, 1, 0))
    east = jnp.where(lane == YB - 1, right, pltpu.roll(v, YB - 1, 1))
    west = jnp.where(lane == 0, left, pltpu.roll(v, 1, 1))
    return down + up + east + west - 4.0 * v


def rim(f, z, depth, rows_lo, rows_hi, cols_lo, cols_hi):
    spot = f * depth + z
    above = jnp.broadcast_to(rows_lo[f, pl.ds(z, 1), :], (XB, YB))
    below = jnp.broadcast_to(rows_hi[f, pl.ds(z, 1), :], (XB, YB))
    left = pltpu.roll(cols_lo[...], (YB - spot) % YB, 1)
    right = pltpu.roll(cols_hi[...], YB - 1 - spot, 1)
    return above, below, left, right


def backward(features, h1, h2, dl, mid, w_out_t, w_temps):
    tops = [nn(w_out_t[g * GROUP : (g + 1) * GROUP], dl) for g in range(WIDE // GROUP)]
    yield
    dh2, lower = [], []
    for top, h in zip(tops, blocks(h2)):
        h = h.astype(F32)
        dh2.append((top * (1.0 - h * h)).astype(BF))
        lower.append(nn(mid[1], dh2[-1]))
        yield
    dh1 = []
    for top, h in zip(lower, blocks(h1)):
        h = h.astype(F32)
        dh1.append((top * (1.0 - h * h)).astype(BF))
        yield
    dh1, dh2 = jnp.concatenate(dh1, axis=0), jnp.concatenate(dh2, axis=0)
    temps = nn(w_temps[...], dh1)
    one_rows = jnp.ones((16, 2 * YB), BF)
    left = jnp.concatenate(
        [jnp.concatenate([h1[x * HID : (x + 1) * HID], one_rows], axis=0) for x in range(XB)], axis=1
    )
    right = jnp.concatenate([dh2[x * HID : (x + 1) * HID] for x in range(XB)], axis=1)
    terms = nt(features, dh1), nt(left, right), nt(dl, h2)
    yield
    return temps, *terms


def steps_kernel(
    desc, solid, fluid, material, fixed, cond_s, cond_f, cot_s, cot_f, push,
    rows_lo, rows_hi, cols_lo, cols_hi,
    h1_ref, h2_ref, logits_ref, first, mid, out, bias, w_in, b_out,
    part, later_push, row_lo, row_hi, col_lo, col_hi, payload,
    w_out_t, w_temps, acc_in, acc_mid, acc_out, acc_dl,
):
    depth = solid.shape[0]
    eye = (iota((2 * XB, 2 * XB), 0) == iota((2 * XB, 2 * XB), 1)).astype(F32).astype(BF)
    w_out_t[...] = tn(out[...], eye).astype(BF)
    pick = ((iota((HID, WIDE), 1) - iota((HID, WIDE), 0)) % HID == 0).astype(F32).astype(BF)
    spread = nn(w_in[...].astype(F32)[DESC:].astype(BF), pick)
    place = (iota((XB, WIDE), 1) // HID) == iota((XB, WIDE), 0)
    for k in range(2):
        line = jnp.broadcast_to(spread[k : k + 1], (XB, WIDE))
        w_temps[k * XB : (k + 1) * XB, :] = jnp.where(place, line, 0.0).astype(BF)
    acc_in[...] = jnp.zeros_like(acc_in)
    acc_mid[...] = jnp.zeros_like(acc_mid)
    acc_out[...] = jnp.zeros_like(acc_out)
    acc_dl[...] = jnp.zeros_like(acc_dl)

    def stream(pair):
        zs = [2 * pair + k for k in range(2)]
        rims = (rows_lo, rows_hi, cols_lo, cols_hi)
        weight = [time_step * (1.0 - fixed[z].astype(F32)) for z in zs]
        k_s = [lookup(material[z], cond_s) for z in zs]
        k_f = [lookup(material[z], cond_f) for z in zs]
        s0 = [solid[z] for z in zs]
        f0 = [fluid[z] for z in zs]
        h_first, h_slope = softplus_terms(logits_ref[pair, 0])
        a_first, a_slope = softplus_terms(logits_ref[pair, 1])
        c0 = h_first * a_first
        lap_s = [laplace(s0[k], *rim(0, zs[k], depth, *rims)) for k in range(2)]
        lap_f = [laplace(f0[k], *rim(1, zs[k], depth, *rims)) for k in range(2)]
        weight, k_s, k_f = wide(weight), wide(k_s), wide(k_f)
        s0w, f0w = wide(s0), wide(f0)
        gap0 = f0w - s0w
        swing = c0 * gap0
        s1 = s0w + weight * (k_s * wide(lap_s) + swing)
        f1 = f0w + weight * (k_f * wide(lap_f) - swing)

        features1 = features_of(desc, (s1[:, :YB], s1[:, YB:]), (f1[:, :YB], f1[:, YB:]), pair)
        g1, g2, l0, l1 = yield from forward(features1, first, mid, out, bias, b_out)
        h_sf, h_sl = softplus_terms(l0)
        a_sf, a_sl = softplus_terms(l1)
        gs, gf = wide([cot_s[z] for z in zs]), wide([cot_f[z] for z in zs])
        us, uf = weight * gs, weight * gf
        dcoup = (f1 - s1) * (us - uf)
        dl = jnp.concatenate([dcoup * a_sf * h_sl, dcoup * h_sf * a_sl], axis=0).astype(BF)
        temps, t_in, t_mid, t_out = yield from backward(features1, g1, g2, dl, mid, w_out_t, w_temps)
        lap_s = wide([laplace(push[0, z], *rim(2, z, depth, *rims)) for z in zs])
        lap_f = wide([laplace(push[1, z], *rim(3, z, depth, *rims)) for z in zs])
        swing = h_sf * a_sf * (uf - us)
        gs = gs + lap_s + swing + temps[:XB]
        gf = gf + lap_f - swing + temps[XB:]

        us, uf = weight * gs, weight * gf
        ps, pf = k_s * us, k_f * uf
        dcoup = gap0 * (us - uf)
        dl0 = jnp.concatenate([dcoup * a_first * h_slope, dcoup * h_first * a_slope], axis=0).astype(BF)
        features0 = features_of(desc, s0, f0, pair)
        temps, u_in, u_mid, u_out = yield from backward(
            features0, h1_ref[pair], h2_ref[pair], dl0, mid, w_out_t, w_temps
        )
        swing = c0 * (uf - us)
        gs = gs + swing + temps[:XB]
        gf = gf - swing + temps[XB:]
        for k in range(2):
            lanes = slice(k * YB, (k + 1) * YB)
            part[0, zs[k]] = gs[:, lanes]
            part[1, zs[k]] = gf[:, lanes]
            later_push[0, zs[k]] = ps[:, lanes]
            later_push[1, zs[k]] = pf[:, lanes]
        acc_in[...] += t_in + u_in
        acc_mid[...] += t_mid + u_mid
        acc_out[...] += t_out + u_out
        acc_dl[...] += dl.astype(F32) + dl0.astype(F32)

    def one(step, _):
        lockstep([stream(STREAMS * step + k) for k in range(STREAMS)])
        return 0

    lax.fori_loop(0, depth // 2 // STREAMS, one, 0)

    for f in range(2):
        row_lo[f] = later_push[f, :, 0, :]
        row_hi[f] = later_push[f, :, XB - 1, :]
    pack_columns([lambda z, f=f: later_push[f, z] for f in range(2)], depth, col_lo, col_hi)

    def diagonal(acc, blocks):
        same = (iota((XB, WIDE), 1) // HID) == iota((XB, WIDE), 0)
        lines = []
        for b in range(blocks):
            kept = jnp.where(same, acc[b * XB : (b + 1) * XB, :], 0.0)
            lines.append(jnp.sum(kept, axis=0, keepdims=True))
        lines = jnp.concatenate(lines, axis=0)
        total = lines[:, :YB]
        for j in range(1, WIDE // YB):
            total = total + lines[:, j * YB : (j + 1) * YB]
        return total[:, :HID] + total[:, HID:]

    half = HID // 2
    grads = payload.at[0]
    grads[:half, :HID] = acc_mid[:half, :]
    grads[:half, HID:] = acc_mid[half:HID, :]
    grads[half:, :] = jnp.zeros((16, YB), F32)
    grads[half : half + 13, :HID] = diagonal(acc_in, 13)
    grads[half : half + 1, HID:] = acc_mid[HID : HID + 1, :]
    grads[half + 1 : half + 3, HID:] = diagonal(acc_out, 2)
    dl_rows = jnp.sum(acc_dl[...], axis=1, keepdims=True)
    for k in range(2):
        total = jnp.sum(dl_rows[k * XB : (k + 1) * XB], axis=0, keepdims=True)
        grads[half + 3 + k : half + 4 + k, HID:] = jnp.broadcast_to(total, (1, HID))
    for copy in range(1, payload.shape[0]):
        payload[copy] = payload[0]


def finish_kernel(
    scale, part, push, rows_lo, rows_hi, cols_lo, cols_hi, summed,
    adj_s, adj_f, g_w_in, g_b_in, g_w_mid, g_b_mid, g_w_out, g_b_out,
):
    depth = part.shape[1]
    rims = (rows_lo, rows_hi, cols_lo, cols_hi)

    def one(z, _):
        for f, adj in enumerate((adj_s, adj_f)):
            adj[z] = part[f, z] + laplace(push[f, z], *rim(f, z, depth, *rims))
        return 0

    for z in range(depth):
        one(z, 0)
    half = HID // 2
    g_w_mid[:half, :] = summed[:half, :HID] * scale
    g_w_mid[half:, :] = summed[:half, HID:] * scale
    g_w_in[...] = summed[half : half + 12, :HID] * scale
    g_b_in[...] = summed[half + 12 : half + 13, :HID] * scale
    g_b_mid[...] = summed[half : half + 1, HID:] * scale
    g_w_out[...] = summed[half + 1 : half + 3, HID:] * scale
    first = iota((1, HID), 1) == 0
    for k in range(2):
        g_b_out[k] = jnp.sum(jnp.where(first, summed[half + 3 + k : half + 4 + k, HID:], 0.0)) * scale


def shift(value, axis, step):
    count = lax.axis_size(axis)
    pairs = [(i, i + step) for i in range(count) if 0 <= i + step < count]
    return lax.ppermute(value, axis, pairs)


def exchange(row_lo, row_hi, col_lo, col_hi):
    return (
        shift(row_hi, "grp", 1),
        shift(row_lo, "grp", -1),
        shift(col_hi, "col", 1),
        shift(col_lo, "col", -1),
    )


def torus_groups():
    at = lambda x, y, z, core: (2 * z + y % 2) * 32 + 8 * x + 2 * (y // 2) + core
    xs, ys, zs, cores = range(4), range(8), range(8), range(2)
    return (
        [[at(x, y, z, c) for x in xs for c in cores] for y in ys for z in zs],
        [[at(x, y, z, c) for y in ys] for x in xs for z in zs for c in cores],
        [[at(x, y, z, c) for z in zs] for x in xs for y in ys for c in cores],
    )


def rings():
    count = lax.axis_size("grp"), lax.axis_size("col")
    return torus_groups() if count == (16, 32) else ([list(range(count[0] * count[1]))],)


def total_over_devices(copies):
    axes = ("grp", "col")
    for members in rings():
        if copies.ndim == 2:
            copies = jnp.broadcast_to(copies[None], (len(members[0]), *copies.shape))
        copies = lax.all_to_all(copies, axes, 0, 0, axis_index_groups=members).sum(0)
    return copies


def shape(dims, kind=F32):
    return jax.ShapeDtypeStruct(dims, kind)


def shards(
    descriptors, solid_temp, fluid_temp, material, fixed_mask, solid_cond, fluid_cond,
    w_in, b_in, w_mid, b_mid, w_out, b_out, solid_cot, fluid_cot,
):
    depth = solid_temp.shape[0]
    field = (depth, XB, YB)
    rows, column = (4, depth, YB), (XB, YB)
    given = (
        solid_temp, fluid_temp, material, fixed_mask, solid_cot, fluid_cot,
        descriptors, w_in, b_in[None], w_mid, b_mid[None], w_out.T, b_out[None],
    )
    *loaded, row_lo, row_hi, col_lo, col_hi, push = pl.pallas_call(
        edges_kernel,
        out_shape=[pltpu.VMEM(v.shape, v.dtype) for v in given]
        + [shape(rows), shape(rows), shape(column), shape(column), pltpu.VMEM((2,) + field, F32)],
        in_specs=[SMEM] * 2 + [HBM] * LOADED,
        out_specs=[VMEM] * (LOADED + 5),
        scratch_shapes=[pltpu.SemaphoreType.DMA((LOADED,))],
        compiler_params=pltpu.CompilerParams(vmem_limit_bytes=65_050_000),
        name="edges",
    )(solid_cond, fluid_cond, *given)
    edges = row_lo, row_hi, col_lo, col_hi
    solid, fluid, material, fixed, cot_s, cot_f, desc, *weights = loaded
    received = exchange(*edges)

    pairs = depth // 2
    kept = [
        pltpu.VMEM((pairs, WIDE, 2 * YB), BF),
        pltpu.VMEM((pairs, WIDE, 2 * YB), BF),
        pltpu.VMEM((pairs, 2, XB, 2 * YB), F32),
        pltpu.VMEM((WIDE, KF), BF),
        pltpu.VMEM((2, GROUP, GROUP), BF),
        pltpu.VMEM((2 * XB, WIDE), BF),
        pltpu.VMEM((HID, YB), F32),
    ]
    saved = pl.pallas_call(
        forward_kernel,
        out_shape=kept,
        in_specs=[VMEM] * 9,
        out_specs=[VMEM] * len(kept),
        cost_estimate=pl.CostEstimate(flops=2**29, bytes_accessed=2**24, transcendentals=2**22),
        name="forward",
        compiler_params=pltpu.CompilerParams(vmem_limit_bytes=24 * 2**20),
    )(desc, solid, fluid, *weights)

    part, later_push, *edges, payload = pl.pallas_call(
        steps_kernel,
        out_shape=[
            shape((2,) + field),
            shape((2,) + field),
            shape((2, depth, YB)),
            shape((2, depth, YB)),
            shape(column),
            shape(column),
            shape((len(rings()[0][0]), 48, YB)),
        ],
        in_specs=[VMEM] * 5 + [SMEM] * 2 + [VMEM] * 16,
        out_specs=[VMEM] * 7,
        scratch_shapes=[
            pltpu.VMEM((WIDE, 2 * XB), BF),
            pltpu.VMEM((2 * XB, WIDE), BF),
            pltpu.VMEM((KF, WIDE), F32),
            pltpu.VMEM((HID + 16, HID), F32),
            pltpu.VMEM((2 * XB, WIDE), F32),
            pltpu.VMEM((2 * XB, 2 * YB), F32),
        ],
        cost_estimate=pl.CostEstimate(flops=2**31, bytes_accessed=2**24, transcendentals=2**22),
        name="steps",
        compiler_params=pltpu.CompilerParams(vmem_limit_bytes=32 * 2**20),
    )(
        desc, solid, fluid, material, fixed, solid_cond, fluid_cond,
        cot_s, cot_f, push, *received, *saved, weights[0], weights[-1],
    )
    received = exchange(*edges)
    summed = total_over_devices(payload)

    cells = solid_temp.size * lax.axis_size("grp") * lax.axis_size("col")
    scale = loss_gain / math.sqrt(cells)
    adj_s, adj_f, *grads = pl.pallas_call(
        functools.partial(finish_kernel, scale),
        out_shape=[
            shape(field), shape(field),
            shape((12, HID)), shape((1, HID)), shape((HID, HID)), shape((1, HID)),
            shape((2, HID)), shape((2,)),
        ],
        in_specs=[VMEM] * 7,
        out_specs=[VMEM] * 7 + [SMEM],
        name="finish",
        compiler_params=pltpu.CompilerParams(vmem_limit_bytes=16 * 2**20),
    )(part, later_push, *received, summed)
    return (
        adj_s, adj_f, grads[0], grads[1][0], grads[2], grads[3][0], grads[4].T, grads[5],
    )


def solution(mesh):
    field, whole = P(None, "grp", "col"), P()
    placed = (
        (P(None, None, "grp", "col"),) + (field,) * 4 + (whole,) * 8 + (field,) * 2
    )
    return jax.shard_map(
        shards,
        mesh=mesh,
        in_specs=placed,
        out_specs=(field, field) + (whole,) * 6,
        check_vma=False,
    )
```
